32 devices in a mesh: layer: 4 (over y, core), front: 8 (over z, x).
Axes of the slice: x: 2, y: 2, z: 4, core: 2. Of those that a mesh axis runs over, the one named last changes fastest.
Arguments:
- sources_down: float32 [4, 8, 2, 32, 256], P('layer', 'front'), may hold values from -6 to 6
- sources_up: float32 [4, 8, 2, 32, 256], P('layer', 'front'), may hold values from -6 to 6
- leaf_inverse: float32 [4, 8, 2, 256, 256], P('layer', 'front'), may hold values from -0.25 to 0.25
- coupling: float32 [4, 8, 2, 512, 256], P('layer', 'front'), may hold values from -0.25 to 0.25
- sep_inverse: float32 [4, 8, 2, 256, 256], P('layer', 'front'), may hold values from -0.25 to 0.25
- inject_top: float32 [4, 8, 2, 128, 256], P('layer', 'front'), may hold values from -0.125 to 0.125
- inject_bottom: float32 [4, 8, 2, 128, 256], P('layer', 'front'), may hold values from -0.125 to 0.125
- targets: int32 [4, 8, 16, 1], P('layer', 'front'), may hold values from 0 to 7; in each aligned block of 16 rows (0 to 15, 16 to 31, ..., all dimensions but the last counted through in order) at most 2 rows name the same one
- offsets: int32 [4, 8, 16], P('layer', 'front'), may hold values from 0 to 7
Outputs:
- field_down: float32 [4, 8, 2, 32, 256], P('layer', 'front')
- field_up: float32 [4, 8, 2, 32, 256], P('layer', 'front')
The draws below stay inside these ranges and needn't reach their ends.
Inputs may be any that keep to these rules, and one draw needn't show every extreme that they name: `targets`: the 16 blocks of one leaf name one separator at most 2 times, and in every draw some leaf names one separator exactly 2 times.
All inputs are finite; a program needn't handle non-finite values.
Results may differ from the reference program's by a relative error of at most 0.00019.
Values sent between devices are 32-bit elements; how exact they have to be, the bound alone decides.
A program may use at most 64 MiB of HBM per device.

```python
import math
import jax
import jax.numpy as jnp
import numpy as np
from jax import lax

P_SIZE = 256
B = 512
Q = 256
TR = 128
RB = 32
S = 32
NB = 16
QB = 8
CAP = 2
LAYERS = 4
LEAVES = 8


def set_ends(entries, rng, low, high):
    spot = [jax.random.randint(jax.random.fold_in(rng, axis), (), 0, length) for axis, length in enumerate(entries.shape)]
    main_axis = entries.shape.index(max(entries.shape))
    neighbour = spot[:main_axis] + [(spot[main_axis] + 1) % entries.shape[main_axis]] + spot[main_axis + 1:]
    return entries.at[tuple(spot)].set(low).at[tuple(neighbour)].set(high)


def shard_levels(key, dims, pieces, low, high):
    level = 1.0
    for dim, parts in pieces:
        steps = jax.random.uniform(jax.random.fold_in(jax.random.fold_in(key, 6), dim), (parts,), jnp.float32, low / len(pieces), high / len(pieces))
        level = level * jnp.repeat(jnp.exp(steps), dims[dim] // parts).reshape((-1,) + (1,) * (len(dims) - 1 - dim))
    return level


def routed_block(rng, own, number, rows, amount, top, most, lean):
    order = jax.random.permutation(rng, amount)
    crowded, ordinary = portions_of(amount, rows * top, most, lean, True), portions_of(amount, rows * top, most, lean, False)
    places = jnp.arange(amount)

    def named(lengths, turn):
        used = int((lengths > 0).sum())
        fixed = max(1, used // 4)
        passed = fixed + (places - fixed + turn * (used - fixed)) % max(1, amount - fixed)
        return jnp.zeros((amount,), jnp.int32).at[order[jnp.where(places < fixed, places, passed)]].set(jnp.asarray(lengths, jnp.int32))

    lengths = jnp.where(number % 4 == 0, named(crowded, number // 4), named(ordinary, number - number // 4 - 1))
    mixed = jax.random.permutation(jax.random.fold_in(own, 3), amount)
    donor, taker = mixed[0:amount // 2 * 2:2], mixed[1:amount // 2 * 2:2]
    room = jnp.minimum(lengths[donor] - 1, most - lengths[taker]) // 2
    room = jnp.where((donor == order[0]) | (taker == order[0]) | (lengths[taker] == 0), 0, jnp.maximum(room, 0))
    passed = jax.random.randint(jax.random.fold_in(own, 4), (amount // 2,), 0, 1 << 20) % (room + 1)
    lengths = lengths.at[donor].add(-passed).at[taker].add(passed)
    items = jnp.searchsorted(jnp.cumsum(lengths), jnp.arange(rows * top), side="right").astype(jnp.int32)
    listing = items.reshape(top, rows).T
    listing = listing[jax.random.permutation(jax.random.fold_in(own, 1), rows)]
    turn = jax.random.randint(jax.random.fold_in(own, 2), (rows, 1), 0, top)
    return jnp.take_along_axis(listing, (jnp.arange(top)[None, :] + turn) % top, axis=1)


def portions_of(amount, total, bound, lean, full):
    loads = [(1 << 20) // math.isqrt(rank ** lean) + 1 for rank in range(1, amount + 1)]
    largest = bound if full else min(bound, max(-(-total // amount), total * loads[0] // sum(loads)))
    least = 1 if total - largest >= amount - 1 else 0
    holding, rest = [largest] + [least] * (amount - 1), total - largest - least * (amount - 1)
    while rest > 0:
        free = [i for i in range(1, amount) if holding[i] < largest] or [i for i in range(1, amount) if holding[i] < bound]
        pool, budget = sum([loads[i] for i in free]), rest
        for i in free:
            more = min(bound - holding[i], max(1, budget * loads[i] // pool), rest)
            holding[i] = holding[i] + more
            rest = rest - more
    return np.array(holding)


def normal_values(stream_key, extent, deviation, bound, shards=(), kind=jnp.bfloat16):
    gain = shard_levels(stream_key, extent, shards, -0.22, 0.18) if shards else 1.0
    values = jax.random.normal(stream_key, extent, jnp.float32) * deviation * gain
    return jnp.minimum(jnp.maximum(values, -bound), bound).astype(kind)


def setup_inputs(seed: int = 0) -> dict:
    key_list = jax.random.split(jax.random.key(seed), 10)
    sources_down = normal_values(key_list[0], (LAYERS, LEAVES, 2, S, P_SIZE), 1.0, 6.0, ((0, 4), (1, 8)), jnp.float32)
    sources_up = normal_values(key_list[1], (LAYERS, LEAVES, 2, S, P_SIZE), 1.0, 6.0, ((0, 4), (1, 8)), jnp.float32)
    leaf_inverse = normal_values(key_list[2], (LAYERS, LEAVES, 2, P_SIZE, P_SIZE), (2 * P_SIZE) ** -0.5, 0.25, ((0, 4), (1, 8)), jnp.float32)
    coupling = normal_values(key_list[3], (LAYERS, LEAVES, 2, B, P_SIZE), (2 * P_SIZE) ** -0.5, 0.25, ((0, 4), (1, 8)), jnp.float32)
    sep_inverse = normal_values(key_list[4], (LAYERS, LEAVES, 2, Q, Q), (2 * Q) ** -0.5, 0.25, ((0, 4), (1, 8)), jnp.float32)
    inject_top = normal_values(key_list[5], (LAYERS, LEAVES, 2, TR, P_SIZE), (16 * TR) ** -0.5, 0.125, ((0, 4), (1, 8)), jnp.float32)
    inject_bottom = normal_values(key_list[6], (LAYERS, LEAVES, 2, TR, P_SIZE), (16 * TR) ** -0.5, 0.125, ((0, 4), (1, 8)), jnp.float32)
    targets_keys = jax.random.split(jax.random.fold_in(key_list[7], 1), LAYERS * LEAVES * NB // NB)
    targets_turns = jax.random.permutation(jax.random.fold_in(key_list[7], 3), LAYERS * LEAVES * NB // NB)
    targets = jax.vmap(lambda own, number: routed_block(jax.random.fold_in(key_list[7], 2), own, number, NB, LEAVES, 1, CAP, 2))(targets_keys, targets_turns).reshape((LAYERS, LEAVES, NB, 1))
    offsets = set_ends(jax.random.randint(key_list[8], (LAYERS, LEAVES, NB), 0, QB), jax.random.fold_in(key_list[8], 1), 0, QB - 1).astype(jnp.int32)
    return dict(sources_down=sources_down, sources_up=sources_up, leaf_inverse=leaf_inverse, coupling=coupling, sep_inverse=sep_inverse, inject_top=inject_top, inject_bottom=inject_bottom, targets=targets, offsets=offsets)


precise = lax.Precision.HIGHEST


def complex_product(pattern, first, second):
    real_part = jnp.einsum(pattern, first[0], second[0], precision=precise) - jnp.einsum(pattern, first[1], second[1], precision=precise)
    imag_part = jnp.einsum(pattern, first[0], second[1], precision=precise) + jnp.einsum(pattern, first[1], second[0], precision=precise)
    return real_part, imag_part


def layer_solve(rhs_pair, leaf_matrix, coupling_rows, sep_matrix, target_list, offset_list):
    leaves = rhs_pair[0].shape[0]
    columns = rhs_pair[0].shape[1]
    leaf_pair = (leaf_matrix[:, 0], leaf_matrix[:, 1])
    coupling_pair = (coupling_rows[:, 0], coupling_rows[:, 1])
    interior = complex_product("fcq,fpq->fcp", rhs_pair, leaf_pair)
    update = complex_product("fcp,fbp->fbc", interior, coupling_pair)
    position = (target_list.astype(jnp.int32) * QB + offset_list.astype(jnp.int32)).reshape(-1).astype(jnp.int32)

    def assemble(part):
        blocks = part.reshape(leaves * NB, RB, columns)
        return jax.ops.segment_sum(blocks, position, num_segments=leaves * QB).reshape(leaves, Q, columns)

    sep_rhs = (assemble(update[0]), assemble(update[1]))
    sep_pair = (sep_matrix[:, 0], sep_matrix[:, 1])
    solved = complex_product("fqc,fpq->fpc", sep_rhs, sep_pair)

    def fetch(part):
        return part.reshape(leaves * QB, RB, columns)[position].reshape(leaves, B, columns)

    returned = (fetch(solved[0]), fetch(solved[1]))
    pushed = complex_product("fbc,fbp->fcp", returned, coupling_pair)
    correction = complex_product("fcq,fpq->fcp", pushed, leaf_pair)
    return interior[0] + correction[0], interior[1] + correction[1]


def sweep(sources, inject, leaf_inverse, coupling, sep_inverse, targets, offsets, order, upward):
    leaves = sources.shape[1]
    blank = jnp.zeros((leaves, S, TR), sources.dtype)
    trace = (blank, blank)
    fields = {}
    for depth_index in order:
        mapping = inject[depth_index]
        injected = complex_product("fct,ftp->fcp", trace, (mapping[:, 0], mapping[:, 1]))
        rhs_pair = (sources[depth_index][:, 0] + injected[0], sources[depth_index][:, 1] + injected[1])
        field = layer_solve(rhs_pair, leaf_inverse[depth_index], coupling[depth_index], sep_inverse[depth_index], targets[depth_index][:, :, 0], offsets[depth_index])
        fields[depth_index] = jnp.stack(field, axis=1)
        if upward:
            trace = (field[0][:, :, :TR], field[1][:, :, :TR])
        else:
            trace = (field[0][:, :, P_SIZE - TR:], field[1][:, :, P_SIZE - TR:])
    return jnp.stack([fields[index] for index in range(sources.shape[0])])


def reference(sources_down, sources_up, leaf_inverse, coupling, sep_inverse, inject_top, inject_bottom, targets, offsets):
    layers = sources_down.shape[0]
    field_down = sweep(sources_down, inject_top, leaf_inverse, coupling, sep_inverse, targets, offsets, list(range(layers)), False)
    field_up = sweep(sources_up, inject_bottom, leaf_inverse, coupling, sep_inverse, targets, offsets, list(range(layers - 1, -1, -1)), True)
    return field_down, field_up
```

```python
import functools

import jax
import jax.numpy as jnp
from jax import lax
from jax.experimental import pallas as pl
from jax.experimental.pallas import tpu as pltpu
from jax.sharding import PartitionSpec as P

CAP = 2
F32 = jnp.float32
BF16 = jnp.bfloat16


def split(x):
    hi = x.astype(BF16)
    return hi, (x - hi.astype(F32)).astype(BF16)


def mm(a, b, rhs_dim=0):
    return lax.dot_general(a, b, (((1,), (rhs_dim,)), ((), ())), preferred_element_type=F32)


def dot3(a, b, rhs_dim=0):
    return mm(a[0], b[0], rhs_dim) + (mm(a[0], b[1], rhs_dim) + mm(a[1], b[0], rhs_dim))


def turned(x):
    half = x.shape[1] // 2
    return jnp.concatenate([-x[:, half:], x[:, :half]], axis=1)


def apply(w_hi, w_lo, x):
    n = x.shape[1]
    hi, lo = split(jnp.concatenate([x, turned(x)], axis=0))
    p = mm(w_hi, jnp.concatenate([hi, lo], axis=1))
    return p[:, :n] + p[:, n:] + mm(w_lo, hi)


def twin(cat):
    half = cat.shape[1] // 2
    re, im = cat[:, :half], cat[:, half:]
    return jnp.concatenate(
        [jnp.concatenate([re, -im], axis=1), jnp.concatenate([im, re], axis=1)], axis=0
    )


def kernel(
    leaves, depth,
    tgt, off, s_down, s_up, leaf, coup, sep, j_top, j_bot,
    out_down, out_up,
    lw, cw, sw, jw, m1, m2, ybuf, ubuf, msend, marr, usend, uarr, rsend, rarr, tsend, tarr,
    ms, mr, us, ur, rs, rr, ts, tr,
):
    layer, me = lax.axis_index("layer"), lax.axis_index("front")
    nb, rb, psize = coup.shape[1:]
    qsize = sep.shape[1]
    qb = qsize // rb
    cols = s_down.shape[1]
    tsize = j_top.shape[1]
    lanes = 2 * cols
    width = CAP * lanes
    slots = leaves * CAP

    barrier = pltpu.get_barrier_semaphore()
    for i in range(1, leaves):
        pl.semaphore_signal(
            barrier, inc=1, device_id={"front": lax.rem(me + i, leaves)}, device_id_type=pl.DeviceIdType.MESH
        )
    inward, onward = layer > 0, layer < depth - 1
    inner = jnp.logical_and(inward, onward)

    @pl.when(inward)
    def _():
        pl.semaphore_signal(barrier, inc=1, device_id={"layer": layer - 1}, device_id_type=pl.DeviceIdType.MESH)

    @pl.when(onward)
    def _():
        pl.semaphore_signal(barrier, inc=1, device_id={"layer": layer + 1}, device_id_type=pl.DeviceIdType.MESH)

    first = lax.div(2 * layer, depth)
    way = (first, 1 - first)

    t = [tgt[n] for n in range(nb)]
    o = [off[n] for n in range(nb)]
    slot = []
    for n in range(nb):
        rank = jnp.int32(0)
        for m in range(n):
            rank = rank + jnp.where(t[m] == t[n], 1, 0)
        slot.append(t[n] * CAP + rank)
    lane = lax.broadcasted_iota(jnp.int32, (qb, width), 1)
    row = lax.broadcasted_iota(jnp.int32, (qb, width), 0)
    for p in range(2):
        hi, lo = split(leaf[p])
        lw[0, :, p * psize:(p + 1) * psize] = hi
        lw[1, :, p * psize:(p + 1) * psize] = lo
    for s in range(leaves):
        place = jnp.full((qb, width), -1, jnp.int32)
        for c in range(CAP):
            k = s * CAP + c
            block, count, where = jnp.int32(0), jnp.int32(0), jnp.int32(0)
            for n in range(nb):
                hit = slot[n] == k
                block = block + jnp.where(hit, n, 0)
                count = count + jnp.where(hit, 1, 0)
                where = where + jnp.where(hit, o[n], 0)
            where = jnp.where(count > 0, where, -1)
            place = jnp.where(lax.div(lane, lanes) == c, where, place)
            keep = count.astype(F32)
            for p in range(2):
                hi, lo = split(coup[p, block] * keep)
                cw[0, k * rb:(k + 1) * rb, p * psize:(p + 1) * psize] = hi
                cw[1, k * rb:(k + 1) * rb, p * psize:(p + 1) * psize] = lo
        msend[s] = jnp.where(row == place, 1.0, 0.0).astype(F32)
    marr[me] = msend[me]

    def prepare(e):
        up = way[e] > 0
        g = jnp.where(up, s_up[...], s_down[...]).reshape(2 * cols, psize).T
        y = apply(lw[0], lw[1], g)
        ybuf[e] = y
        ubuf[e] = apply(cw[0], cw[1], y)

    prepare(0)

    def across(src, dst, send, recv, i, tag):
        there, back = lax.rem(me + i, leaves), lax.rem(me + leaves - i, leaves)
        kind = pl.DeviceIdType.MESH
        out = pltpu.make_async_remote_copy(
            src.at[tag + (there,)], dst.at[tag + (me,)], send.at[tag + (there,)], recv.at[tag + (me,)],
            device_id={"front": there}, device_id_type=kind)
        into = pltpu.make_async_remote_copy(
            src.at[tag + (back,)], dst.at[tag + (back,)], send.at[tag + (back,)], recv.at[tag + (back,)],
            device_id={"front": back}, device_id_type=kind)
        return out, into

    mask_moves = [across(msend, marr, ms, mr, i, ()) for i in range(1, leaves)]
    u_moves = [[across(usend, uarr, us, ur, i, (e,)) for i in range(1, leaves)] for e in range(2)]
    r_moves = [[across(rsend, rarr, rs, rr, i, (e,)) for i in range(1, leaves)] for e in range(2)]

    def trace_move(e):
        d = way[e]
        return pltpu.make_async_remote_copy(
            tsend.at[d], tarr.at[d], ts.at[d], tr.at[d],
            device_id={"layer": layer + 1 - 2 * d}, device_id_type=pl.DeviceIdType.MESH)

    def arrived_trace(e):
        d = way[e]
        pltpu.make_async_remote_copy(
            tsend.at[d], tarr.at[d], ts.at[d], tr.at[d],
            device_id={"layer": layer - 1 + 2 * d}, device_id_type=pl.DeviceIdType.MESH).wait_recv()
        held = tarr[d]
        return jnp.concatenate([held[:, :lanes], held[:, lanes:]], axis=0)

    def send_update(e, u):
        for s in range(leaves):
            usend[e, s] = jnp.concatenate(
                [u[(s * CAP + c) * rb:(s * CAP + c + 1) * rb] for c in range(CAP)], axis=1)
        for out, _ in u_moves[e]:
            out.start()
        uarr[e, me] = usend[e, me]

    def with_trace(e):
        d = way[e]
        trace = arrived_trace(e)
        send_update(e, ubuf[e] + apply(m1[0, d], m1[1, d], trace))
        ybuf[e] = ybuf[e] + apply(jw[0, d], jw[1, d], trace)

    pl.semaphore_wait(barrier, leaves - 1 + jnp.where(inward, 1, 0) + jnp.where(onward, 1, 0))
    for out, _ in mask_moves:
        out.start()

    @pl.when(jnp.logical_not(inner))
    def _():
        send_update(0, ubuf[0])

    for p in range(2):
        hi, lo = split(sep[p])
        sw[0, :, p * qsize:(p + 1) * qsize] = hi
        sw[1, :, p * qsize:(p + 1) * qsize] = lo
    for d, inject in enumerate((j_top, j_bot)):
        mapping = twin(jnp.concatenate([inject[0], inject[1]], axis=1))
        lj = dot3((lw[0], lw[1]), split(mapping), 1)
        jw[0, d], jw[1, d] = split(lj)
        ljr, lji = lj[:, :tsize], lj[:, tsize:]
        grid = jnp.concatenate(
            [jnp.concatenate([ljr, lji], axis=1), jnp.concatenate([-lji, ljr], axis=1)], axis=0)
        m1[0, d], m1[1, d] = split(dot3((cw[0], cw[1]), split(grid)))

    @pl.when(inner)
    def _():
        with_trace(0)

    for e in range(2):
        d = way[e]
        if e == 1:
            with_trace(1)
        else:
            for _, into in mask_moves:
                into.wait_recv()
        for _, into in u_moves[e]:
            into.wait_recv()
        blocks = []
        for b in range(qb):
            total = uarr[e, 0] * marr[0, b:b + 1]
            for s in range(1, leaves):
                total = total + uarr[e, s] * marr[s, b:b + 1]
            part = total[:, :lanes]
            for c in range(1, CAP):
                part = part + total[:, c * lanes:(c + 1) * lanes]
            blocks.append(part)
        x = apply(sw[0], sw[1], jnp.concatenate(blocks, axis=0))
        wide = [jnp.concatenate([x[b * rb:(b + 1) * rb]] * CAP, axis=1) for b in range(qb)]
        for s in range(leaves):
            total = wide[0] * marr[s, 0:1]
            for b in range(1, qb):
                total = total + wide[b] * marr[s, b:b + 1]
            rsend[e, s] = total
        for out, _ in r_moves[e]:
            out.start()
        rarr[e, me] = rsend[e, me]
        if e == 0:
            chi, clo = twin(cw[0]), twin(cw[1])
            m2[0], m2[1] = split(dot3((lw[0], lw[1]), (chi, clo), 1))
            prepare(1)
        for _, into in r_moves[e]:
            into.wait_recv()
        w = jnp.concatenate(
            [rarr[e, s][:, c * lanes:(c + 1) * lanes] for s in range(leaves) for c in range(CAP)], axis=0)

        def pass_on():
            rows = pl.ds(pl.multiple_of((1 - d) * (psize - tsize), 8), tsize)
            trace = ybuf[e, rows] + apply(m2[0, rows], m2[1, rows], w)
            tsend[d] = jnp.concatenate([trace[:tsize // 2], trace[tsize // 2:]], axis=1)
            trace_move(e).start()

        if e == 0:
            pass_on()
        else:
            pl.when(inner)(pass_on)
        field = (ybuf[e] + apply(m2[0], m2[1], w)).T.reshape(2, cols, psize)

        @pl.when(d == 0)
        def _():
            out_down[...] = field

        @pl.when(d == 1)
        def _():
            out_up[...] = field

    for moves in [mask_moves] + u_moves + r_moves:
        for out, _ in moves:
            out.wait_send()
    trace_move(0).wait_send()

    @pl.when(inner)
    def _():
        trace_move(1).wait_send()


def solution(mesh):
    leaves, depth = mesh.shape["front"], mesh.shape["layer"]

    def body(s_down, s_up, leaf, coup, sep, j_top, j_bot, targets, offsets):
        cols, psize = s_down.shape[3:]
        nb = offsets.shape[2]
        bsize, qsize, tsize = coup.shape[3], sep.shape[3], j_top.shape[3]
        rb = bsize // nb
        qb = qsize // rb
        lanes = 2 * cols
        width = CAP * lanes
        rows = leaves * CAP * rb
        vmem = pl.BlockSpec(memory_space=pltpu.VMEM)
        smem = pl.BlockSpec(memory_space=pltpu.SMEM)
        sems = pltpu.SemaphoreType.DMA
        field = jax.ShapeDtypeStruct((2, cols, psize), F32)
        down, up = pl.pallas_call(
            functools.partial(kernel, leaves, depth),
            out_shape=(field, field),
            in_specs=[smem] * 2 + [vmem] * 7,
            out_specs=(vmem, vmem),
            scratch_shapes=[
                pltpu.VMEM((2, psize, 2 * psize), BF16),
                pltpu.VMEM((2, rows, 2 * psize), BF16),
                pltpu.VMEM((2, qsize, 2 * qsize), BF16),
                pltpu.VMEM((2, 2, psize, 2 * tsize), BF16),
                pltpu.VMEM((2, 2, rows, 2 * tsize), BF16),
                pltpu.VMEM((2, psize, 2 * rows), BF16),
                pltpu.VMEM((2, psize, lanes), F32),
                pltpu.VMEM((2, rows, lanes), F32),
                pltpu.VMEM((leaves, qb, width), F32),
                pltpu.VMEM((leaves, qb, width), F32),
                pltpu.VMEM((2, leaves, rb, width), F32),
                pltpu.VMEM((2, leaves, rb, width), F32),
                pltpu.VMEM((2, leaves, rb, width), F32),
                pltpu.VMEM((2, leaves, rb, width), F32),
                pltpu.VMEM((2, tsize // 2, 2 * lanes), F32),
                pltpu.VMEM((2, tsize // 2, 2 * lanes), F32),
                sems((leaves,)), sems((leaves,)),
                sems((2, leaves)), sems((2, leaves)),
                sems((2, leaves)), sems((2, leaves)),
                sems((2,)), sems((2,)),
            ],
            compiler_params=pltpu.CompilerParams(
                collective_id=0, has_side_effects=True, vmem_limit_bytes=56 * 1024 * 1024
            ),
        )(
            targets.reshape(nb), offsets.reshape(nb),
            s_down[0, 0], s_up[0, 0], leaf[0, 0], coup[0, 0].reshape(2, nb, rb, psize),
            sep[0, 0], j_top[0, 0], j_bot[0, 0],
        )
        return down[None, None], up[None, None]

    five, four, three = (P("layer", "front", *([None] * k)) for k in (3, 2, 1))
    return jax.shard_map(
        body, mesh=mesh, in_specs=(five,) * 7 + (four, three), out_specs=(five, five), check_vma=False
    )
```

```python
import functools

import jax
import jax.numpy as jnp
from jax import lax
from jax.experimental import pallas as pl
from jax.experimental.pallas import tpu as pltpu
from jax.sharding import PartitionSpec as P

CAP = 2
F32 = jnp.float32
BF16 = jnp.bfloat16


def split(x):
    hi = x.astype(BF16)
    return hi, (x - hi.astype(F32)).astype(BF16)


def mm(a, b, rhs_dim=0):
    return lax.dot_general(a, b, (((1,), (rhs_dim,)), ((), ())), preferred_element_type=F32)


def dot3(a, b, rhs_dim=0):
    return mm(a[0], b[0], rhs_dim) + (mm(a[0], b[1], rhs_dim) + mm(a[1], b[0], rhs_dim))


def lanes_of(x):
    return lax.broadcasted_iota(jnp.int32, x.shape, 1)


def turned(x, cols):
    real = lax.rem(lanes_of(x), 2 * cols) < cols
    return jnp.where(real, -pltpu.roll(x, x.shape[1] - cols, 1), pltpu.roll(x, cols, 1))


def apply(w_hi, w_lo, x, cols):
    n = x.shape[1]
    hi, lo = split(jnp.concatenate([x, turned(x, cols)], axis=0))
    p = mm(w_hi, jnp.concatenate([hi, lo], axis=1))
    return p[:, :n] + p[:, n:] + mm(w_lo, hi)


def pick(parts, group):
    which = lax.div(lanes_of(parts[0]), group)
    out = parts[0]
    for c in range(1, len(parts)):
        out = jnp.where(which == c, parts[c], out)
    return out


def folded(x, group):
    out = x
    for c in range(1, x.shape[1] // group):
        out = out + pltpu.roll(x, c * group, 1)
    return out


def twin(cat):
    half = cat.shape[1] // 2
    re, im = cat[:, :half], cat[:, half:]
    return jnp.concatenate(
        [jnp.concatenate([re, -im], axis=1), jnp.concatenate([im, re], axis=1)], axis=0
    )


def kernel(
    leaves, depth,
    tgt, off, s_down, s_up, leaf, coup, sep_far, top_far, bot_far,
    out_down, out_up,
    sep, j_top, j_bot,
    lw, cw, sw, jw, m1, m2, ybuf, ubuf, msend, marr, usend, uarr, rsend, rarr, tsend, tarr,
    ls, ms, mr, us, ur, rs, rr, ts, tr,
):
    loads = [
        pltpu.make_async_copy(far, near, ls.at[i])
        for i, (far, near) in enumerate(((sep_far, sep), (top_far, j_top), (bot_far, j_bot)))
    ]
    for load in loads:
        load.start()
    layer, me = lax.axis_index("layer"), lax.axis_index("front")
    nb, rb, psize = coup.shape[1:]
    qsize = sep.shape[1]
    qb = qsize // rb
    cols = s_down.shape[1]
    tsize = j_top.shape[1]
    lanes = 2 * cols
    width = CAP * lanes
    wide = leaves * rb
    apply_c = functools.partial(apply, cols=cols)

    barrier = pltpu.get_barrier_semaphore()
    for i in range(1, leaves):
        pl.semaphore_signal(
            barrier, inc=1, device_id={"front": lax.rem(me + i, leaves)}, device_id_type=pl.DeviceIdType.MESH
        )
    inward, onward = layer > 0, layer < depth - 1
    inner = jnp.logical_and(inward, onward)

    @pl.when(inward)
    def _():
        pl.semaphore_signal(barrier, inc=1, device_id={"layer": layer - 1}, device_id_type=pl.DeviceIdType.MESH)

    @pl.when(onward)
    def _():
        pl.semaphore_signal(barrier, inc=1, device_id={"layer": layer + 1}, device_id_type=pl.DeviceIdType.MESH)

    first = lax.div(2 * layer, depth)
    way = (first, 1 - first)

    t = [tgt[n] for n in range(nb)]
    o = [off[n] for n in range(nb)]
    slot = []
    for n in range(nb):
        rank = jnp.int32(0)
        for m in range(n):
            rank = rank + jnp.where(t[m] == t[n], 1, 0)
        slot.append(t[n] * CAP + rank)
    lane = lax.broadcasted_iota(jnp.int32, (qb, width), 1)
    row = lax.broadcasted_iota(jnp.int32, (qb, width), 0)
    for p in range(2):
        hi, lo = split(leaf[p])
        lw[0, :, p * psize:(p + 1) * psize] = hi
        lw[1, :, p * psize:(p + 1) * psize] = lo
    for s in range(leaves):
        place = jnp.full((qb, width), -1, jnp.int32)
        for c in range(CAP):
            k, at = s * CAP + c, c * leaves + s
            block, count, where = jnp.int32(0), jnp.int32(0), jnp.int32(0)
            for n in range(nb):
                hit = slot[n] == k
                block = block + jnp.where(hit, n, 0)
                count = count + jnp.where(hit, 1, 0)
                where = where + jnp.where(hit, o[n], 0)
            where = jnp.where(count > 0, where, -1)
            place = jnp.where(lax.div(lane, lanes) == c, where, place)
            keep = count.astype(F32)
            for p in range(2):
                hi, lo = split(coup[p, block] * keep)
                cw[0, at * rb:(at + 1) * rb, p * psize:(p + 1) * psize] = hi
                cw[1, at * rb:(at + 1) * rb, p * psize:(p + 1) * psize] = lo
        msend[s] = jnp.where(row == place, 1.0, 0.0).astype(F32)
    marr[me] = msend[me]

    def packed(u):
        return pick([u[c * wide:(c + 1) * wide] for c in range(CAP)], lanes)

    def prepare(e):
        up = way[e] > 0
        g = jnp.where(up, s_up[...], s_down[...]).reshape(lanes, psize)
        y = apply_c(lw[0], lw[1], jnp.concatenate([g] * CAP, axis=0).T)
        ybuf[e] = y
        ubuf[e] = packed(apply_c(cw[0], cw[1], y))

    prepare(0)

    side = 2 * lax.div(2 * me, leaves) - 1

    def across(src, dst, send, recv, i, tag):
        there = lax.rem(me + leaves + side * i, leaves)
        back = there
        kind = pl.DeviceIdType.MESH
        out = pltpu.make_async_remote_copy(
            src.at[tag + (there,)], dst.at[tag + (me,)], send.at[tag + (there,)], recv.at[tag + (me,)],
            device_id={"front": there}, device_id_type=kind)
        into = pltpu.make_async_remote_copy(
            src.at[tag + (back,)], dst.at[tag + (back,)], send.at[tag + (back,)], recv.at[tag + (back,)],
            device_id={"front": back}, device_id_type=kind)
        return out, into

    mask_moves = [across(msend, marr, ms, mr, i, ()) for i in range(1, leaves)]
    u_moves = [[across(usend, uarr, us, ur, i, (e,)) for i in range(1, leaves)] for e in range(2)]
    r_moves = [[across(rsend, rarr, rs, rr, i, (e,)) for i in range(1, leaves)] for e in range(2)]

    def trace_move(e):
        d = way[e]
        return pltpu.make_async_remote_copy(
            tsend.at[d], tarr.at[d], ts.at[d], tr.at[d],
            device_id={"layer": layer + 1 - 2 * d}, device_id_type=pl.DeviceIdType.MESH)

    def arrived_trace(e):
        d = way[e]
        pltpu.make_async_remote_copy(
            tsend.at[d], tarr.at[d], ts.at[d], tr.at[d],
            device_id={"layer": layer - 1 + 2 * d}, device_id_type=pl.DeviceIdType.MESH).wait_recv()
        held = tarr[d]
        over = pltpu.roll(held, lanes, 1)
        return jnp.concatenate([pick([held, over], lanes), pick([over, held], lanes)], axis=0)

    def send_update(e, u):
        usend[e] = u.reshape(leaves, rb, width)
        for out, _ in u_moves[e]:
            out.start()
        uarr[e, me] = usend[e, me]

    def with_trace(e):
        d = way[e]
        trace = arrived_trace(e)
        send_update(e, ubuf[e] + packed(apply_c(m1[0, d], m1[1, d], trace)))
        ybuf[e] = ybuf[e] + apply_c(jw[0, d], jw[1, d], trace)

    pl.semaphore_wait(barrier, leaves - 1 + jnp.where(inward, 1, 0) + jnp.where(onward, 1, 0))
    for out, _ in mask_moves:
        out.start()

    @pl.when(jnp.logical_not(inner))
    def _():
        send_update(0, ubuf[0])

    for load in loads:
        load.wait()
    for p in range(2):
        hi, lo = split(sep[p])
        sw[0, :, p * qsize:(p + 1) * qsize] = hi
        sw[1, :, p * qsize:(p + 1) * qsize] = lo
    for d, inject in enumerate((j_top, j_bot)):
        mapping = twin(jnp.concatenate([inject[0], inject[1]], axis=1))
        lj = dot3((lw[0], lw[1]), split(mapping), 1)
        jw[0, d], jw[1, d] = split(lj)
        ljr, lji = lj[:, :tsize], lj[:, tsize:]
        grid = jnp.concatenate(
            [jnp.concatenate([ljr, lji], axis=1), jnp.concatenate([-lji, ljr], axis=1)], axis=0)
        m1[0, d], m1[1, d] = split(dot3((cw[0], cw[1]), split(grid)))

    @pl.when(inner)
    def _():
        with_trace(0)

    for e in range(2):
        d = way[e]
        if e == 1:
            with_trace(1)
        else:
            for _, into in mask_moves:
                into.wait_recv()
        total = [uarr[e, me] * marr[me, b:b + 1] for b in range(qb)]
        for i in range(leaves - 1, 0, -1):
            u_moves[e][i - 1][1].wait_recv()
            there = lax.rem(me + leaves + side * i, leaves)
            came, mask = uarr[e, there], marr[there]
            total = [total[b] + came * mask[b:b + 1] for b in range(qb)]
        x = apply_c(sw[0], sw[1], jnp.concatenate([folded(part, lanes) for part in total], axis=0))
        for s in range(leaves):
            reply = x[:rb] * marr[s, 0:1]
            for b in range(1, qb):
                reply = reply + x[b * rb:(b + 1) * rb] * marr[s, b:b + 1]
            rsend[e, s] = reply
        for out, _ in r_moves[e]:
            out.start()
        rarr[e, me] = rsend[e, me]
        if e == 0:
            chi, clo = twin(cw[0]), twin(cw[1])
            full = split(dot3((lw[0], lw[1]), (chi, clo), 1))
            for part in range(2):
                for c in range(CAP):
                    for p in range(2):
                        begin = (p * CAP + c) * wide
                        m2[part, c, :, p * wide:(p + 1) * wide] = full[part][:, begin:begin + wide]
            prepare(1)
        for _, into in r_moves[e]:
            into.wait_recv()
        w = rarr[e].reshape(wide, width)
        w_hi, w_lo = split(jnp.concatenate([w, turned(w, cols)], axis=0))
        w_both = jnp.concatenate([w_hi, w_lo], axis=1)

        def corrected(rows):
            parts = []
            for c in range(CAP):
                p = mm(m2[0, c, rows], w_both)
                parts.append(p[:, :width] + p[:, width:] + mm(m2[1, c, rows], w_hi))
            return ybuf[e, rows] + folded(pick(parts, lanes), lanes)

        def pass_on():
            rows = pl.ds(pl.multiple_of((1 - d) * (psize - tsize), 8), tsize)
            trace = corrected(rows)
            tsend[d] = pick([trace[:tsize // 2], trace[tsize // 2:]], lanes)
            trace_move(e).start()

        if e == 0:
            pass_on()
        else:
            pl.when(inner)(pass_on)
        field = corrected(pl.ds(0, psize)).T[:lanes].reshape(2, cols, psize)

        @pl.when(d == 0)
        def _():
            out_down[...] = field

        @pl.when(d == 1)
        def _():
            out_up[...] = field

    for moves in [mask_moves] + u_moves + r_moves:
        for out, _ in moves:
            out.wait_send()
    trace_move(0).wait_send()

    @pl.when(inner)
    def _():
        trace_move(1).wait_send()


def solution(mesh):
    leaves, depth = mesh.shape["front"], mesh.shape["layer"]

    def body(s_down, s_up, leaf, coup, sep, j_top, j_bot, targets, offsets):
        cols, psize = s_down.shape[3:]
        nb = offsets.shape[2]
        bsize, qsize, tsize = coup.shape[3], sep.shape[3], j_top.shape[3]
        rb = bsize // nb
        qb = qsize // rb
        lanes = 2 * cols
        width = CAP * lanes
        rows = leaves * CAP * rb
        vmem = pl.BlockSpec(memory_space=pltpu.VMEM)
        smem = pl.BlockSpec(memory_space=pltpu.SMEM)
        sems = pltpu.SemaphoreType.DMA
        field = jax.ShapeDtypeStruct((2, cols, psize), F32)
        down, up = pl.pallas_call(
            functools.partial(kernel, leaves, depth),
            out_shape=(field, field),
            in_specs=[smem] * 2 + [vmem] * 4 + [pl.BlockSpec(memory_space=pl.ANY)] * 3,
            out_specs=(vmem, vmem),
            scratch_shapes=[
                pltpu.VMEM((2, qsize, qsize), F32),
                pltpu.VMEM((2, tsize, psize), F32),
                pltpu.VMEM((2, tsize, psize), F32),
                pltpu.VMEM((2, psize, 2 * psize), BF16),
                pltpu.VMEM((2, rows, 2 * psize), BF16),
                pltpu.VMEM((2, qsize, 2 * qsize), BF16),
                pltpu.VMEM((2, 2, psize, 2 * tsize), BF16),
                pltpu.VMEM((2, 2, rows, 2 * tsize), BF16),
                pltpu.VMEM((2, CAP, psize, 2 * leaves * rb), BF16),
                pltpu.VMEM((2, psize, width), F32),
                pltpu.VMEM((2, leaves * rb, width), F32),
                pltpu.VMEM((leaves, qb, width), F32),
                pltpu.VMEM((leaves, qb, width), F32),
                pltpu.VMEM((2, leaves, rb, width), F32),
                pltpu.VMEM((2, leaves, rb, width), F32),
                pltpu.VMEM((2, leaves, rb, width), F32),
                pltpu.VMEM((2, leaves, rb, width), F32),
                pltpu.VMEM((2, tsize // 2, 2 * lanes), F32),
                pltpu.VMEM((2, tsize // 2, 2 * lanes), F32),
                sems((3,)),
                sems((leaves,)), sems((leaves,)),
                sems((2, leaves)), sems((2, leaves)),
                sems((2, leaves)), sems((2, leaves)),
                sems((2,)), sems((2,)),
            ],
            compiler_params=pltpu.CompilerParams(
                collective_id=0, has_side_effects=True, vmem_limit_bytes=56 * 1024 * 1024
            ),
        )(
            targets.reshape(nb), offsets.reshape(nb),
            s_down[0, 0], s_up[0, 0], leaf[0, 0], coup[0, 0].reshape(2, nb, rb, psize),
            sep[0, 0], j_top[0, 0], j_bot[0, 0],
        )
        return down[None, None], up[None, None]

    five, four, three = (P("layer", "front", *([None] * k)) for k in (3, 2, 1))
    return jax.shard_map(
        body, mesh=mesh, in_specs=(five,) * 7 + (four, three), out_specs=(five, five), check_vma=False
    )
```

```python
import functools

import jax
import jax.numpy as jnp
from jax import lax
from jax.experimental import pallas as pl
from jax.experimental.pallas import tpu as pltpu
from jax.sharding import PartitionSpec as P

CAP = 2
F32 = jnp.float32
BF16 = jnp.bfloat16


def split(x):
    hi = x.astype(BF16)
    return hi, (x - hi.astype(F32)).astype(BF16)


def mm(a, b, rhs_dim=0):
    return lax.dot_general(a, b, (((1,), (rhs_dim,)), ((), ())), preferred_element_type=F32)


def dot3(a, b, rhs_dim=0):
    return mm(a[0], b[0], rhs_dim) + (mm(a[0], b[1], rhs_dim) + mm(a[1], b[0], rhs_dim))


def lanes_of(x):
    return lax.broadcasted_iota(jnp.int32, x.shape, 1)


def turned(x, cols):
    real = lax.rem(lanes_of(x), 2 * cols) < cols
    return jnp.where(real, -pltpu.roll(x, x.shape[1] - cols, 1), pltpu.roll(x, cols, 1))


def apply(w_hi, w_lo, x, cols):
    n = x.shape[1]
    hi, lo = split(jnp.concatenate([x, turned(x, cols)], axis=0))
    p = mm(w_hi, jnp.concatenate([hi, lo], axis=1))
    return p[:, :n] + p[:, n:] + mm(w_lo, hi)


def pick(parts, group):
    which = lax.div(lanes_of(parts[0]), group)
    out = parts[0]
    for c in range(1, len(parts)):
        out = jnp.where(which == c, parts[c], out)
    return out


def folded(x, group):
    out = x
    for c in range(1, x.shape[1] // group):
        out = out + pltpu.roll(x, c * group, 1)
    return out


def twin(cat):
    half = cat.shape[1] // 2
    re, im = cat[:, :half], cat[:, half:]
    return jnp.concatenate(
        [jnp.concatenate([re, -im], axis=1), jnp.concatenate([im, re], axis=1)], axis=0
    )


def kernel(
    leaves, depth,
    tgt, off, s_down, s_up, leaf, coup, sep_far, top_far, bot_far,
    out,
    sep, j_top, j_bot,
    lw, cw, sw, jw, m1, m2, ybuf, ubuf, msend, marr, usend, uarr, rsend, rarr, tsend, tarr,
    ls, ms, mr, us, ur, rs, rr, ts, tr,
):
    loads = [
        pltpu.make_async_copy(far, near, ls.at[i])
        for i, (far, near) in enumerate(((sep_far, sep), (top_far, j_top), (bot_far, j_bot)))
    ]
    for load in loads:
        load.start()
    layer, me = lax.axis_index("layer"), lax.axis_index("front")
    nb, rb, psize = coup.shape[1:]
    qsize = sep.shape[1]
    qb = qsize // rb
    cols = s_down.shape[1]
    tsize = j_top.shape[1]
    lanes = 2 * cols
    width = CAP * lanes
    wide = leaves * rb
    apply_c = functools.partial(apply, cols=cols)

    barrier = pltpu.get_barrier_semaphore()
    for i in range(1, leaves):
        pl.semaphore_signal(
            barrier, inc=1, device_id={"front": lax.rem(me + i, leaves)}, device_id_type=pl.DeviceIdType.MESH
        )
    inward, onward = layer > 0, layer < depth - 1
    inner = jnp.logical_and(inward, onward)

    @pl.when(inward)
    def _():
        pl.semaphore_signal(barrier, inc=1, device_id={"layer": layer - 1}, device_id_type=pl.DeviceIdType.MESH)

    @pl.when(onward)
    def _():
        pl.semaphore_signal(barrier, inc=1, device_id={"layer": layer + 1}, device_id_type=pl.DeviceIdType.MESH)

    first = lax.div(2 * layer, depth)
    way = (first, 1 - first)

    t = [tgt[n] for n in range(nb)]
    o = [off[n] for n in range(nb)]
    slot = []
    for n in range(nb):
        rank = jnp.int32(0)
        for m in range(n):
            rank = rank + jnp.where(t[m] == t[n], 1, 0)
        slot.append(t[n] * CAP + rank)
    lane = lax.broadcasted_iota(jnp.int32, (qb, width), 1)
    row = lax.broadcasted_iota(jnp.int32, (qb, width), 0)
    for p in range(2):
        hi, lo = split(leaf[p])
        lw[0, :, p * psize:(p + 1) * psize] = hi
        lw[1, :, p * psize:(p + 1) * psize] = lo
    for s in range(leaves):
        place = jnp.full((qb, width), -1, jnp.int32)
        for c in range(CAP):
            k, at = s * CAP + c, c * leaves + s
            block, count, where = jnp.int32(0), jnp.int32(0), jnp.int32(0)
            for n in range(nb):
                hit = slot[n] == k
                block = block + jnp.where(hit, n, 0)
                count = count + jnp.where(hit, 1, 0)
                where = where + jnp.where(hit, o[n], 0)
            where = jnp.where(count > 0, where, -1)
            place = jnp.where(lax.div(lane, lanes) == c, where, place)
            keep = count.astype(F32)
            for p in range(2):
                hi, lo = split(coup[p, block] * keep)
                cw[0, at * rb:(at + 1) * rb, p * psize:(p + 1) * psize] = hi
                cw[1, at * rb:(at + 1) * rb, p * psize:(p + 1) * psize] = lo
        msend[s] = jnp.where(row == place, 1.0, 0.0).astype(F32)
    marr[me] = msend[me]

    def packed(u):
        return pick([u[c * wide:(c + 1) * wide] for c in range(CAP)], lanes)

    def prepare(e):
        up = way[e] > 0
        g = jnp.where(up, s_up[...], s_down[...]).reshape(lanes, psize)
        y = apply_c(lw[0], lw[1], jnp.concatenate([g] * CAP, axis=0).T)
        ybuf[e] = y
        ubuf[e] = packed(apply_c(cw[0], cw[1], y))

    prepare(0)

    side = 2 * lax.div(2 * me, leaves) - 1

    def across(src, dst, send, recv, i, tag):
        there = lax.rem(me + leaves + side * i, leaves)
        back = there
        kind = pl.DeviceIdType.MESH
        out = pltpu.make_async_remote_copy(
            src.at[tag + (there,)], dst.at[tag + (me,)], send.at[tag + (there,)], recv.at[tag + (me,)],
            device_id={"front": there}, device_id_type=kind)
        into = pltpu.make_async_remote_copy(
            src.at[tag + (back,)], dst.at[tag + (back,)], send.at[tag + (back,)], recv.at[tag + (back,)],
            device_id={"front": back}, device_id_type=kind)
        return out, into

    mask_moves = [across(msend, marr, ms, mr, i, ()) for i in range(1, leaves)]
    u_moves = [[across(usend, uarr, us, ur, i, (e,)) for i in range(1, leaves)] for e in range(2)]
    r_moves = [[across(rsend, rarr, rs, rr, i, (e,)) for i in range(1, leaves)] for e in range(2)]

    def trace_move(e):
        d = way[e]
        return pltpu.make_async_remote_copy(
            tsend.at[d], tarr.at[d], ts.at[d], tr.at[d],
            device_id={"layer": layer + 1 - 2 * d}, device_id_type=pl.DeviceIdType.MESH)

    def arrived_trace(e):
        d = way[e]
        pltpu.make_async_remote_copy(
            tsend.at[d], tarr.at[d], ts.at[d], tr.at[d],
            device_id={"layer": layer - 1 + 2 * d}, device_id_type=pl.DeviceIdType.MESH).wait_recv()
        held = tarr[d]
        over = pltpu.roll(held, lanes, 1)
        return jnp.concatenate([pick([held, over], lanes), pick([over, held], lanes)], axis=0)

    def send_update(e, u):
        usend[e] = u.reshape(leaves, rb, width)
        for going, _ in u_moves[e]:
            going.start()
        uarr[e, me] = usend[e, me]

    def with_trace(e):
        d = way[e]
        trace = arrived_trace(e)
        send_update(e, ubuf[e] + packed(apply_c(m1[0, d], m1[1, d], trace)))
        ybuf[e] = ybuf[e] + apply_c(jw[0, d], jw[1, d], trace)

    pl.semaphore_wait(barrier, leaves - 1 + jnp.where(inward, 1, 0) + jnp.where(onward, 1, 0))
    for going, _ in mask_moves:
        going.start()

    @pl.when(jnp.logical_not(inner))
    def _():
        send_update(0, ubuf[0])

    for load in loads:
        load.wait()
    for p in range(2):
        hi, lo = split(sep[p])
        sw[0, :, p * qsize:(p + 1) * qsize] = hi
        sw[1, :, p * qsize:(p + 1) * qsize] = lo
    for d, inject in enumerate((j_top, j_bot)):
        mapping = twin(jnp.concatenate([inject[0], inject[1]], axis=1))
        lj = dot3((lw[0], lw[1]), split(mapping), 1)
        jw[0, d], jw[1, d] = split(lj)
        ljr, lji = lj[:, :tsize], lj[:, tsize:]
        grid = jnp.concatenate(
            [jnp.concatenate([ljr, lji], axis=1), jnp.concatenate([-lji, ljr], axis=1)], axis=0)
        m1[0, d], m1[1, d] = split(dot3((cw[0], cw[1]), split(grid)))

    @pl.when(inner)
    def _():
        with_trace(0)

    for e in range(2):
        d = way[e]
        if e == 1:
            with_trace(1)
        else:
            for _, into in mask_moves:
                into.wait_recv()
        total = [uarr[e, me] * marr[me, b:b + 1] for b in range(qb)]
        for i in range(leaves - 1, 0, -1):
            u_moves[e][i - 1][1].wait_recv()
            there = lax.rem(me + leaves + side * i, leaves)
            came, mask = uarr[e, there], marr[there]
            total = [total[b] + came * mask[b:b + 1] for b in range(qb)]
        x = apply_c(sw[0], sw[1], jnp.concatenate([folded(part, lanes) for part in total], axis=0))
        for s in range(leaves):
            reply = x[:rb] * marr[s, 0:1]
            for b in range(1, qb):
                reply = reply + x[b * rb:(b + 1) * rb] * marr[s, b:b + 1]
            rsend[e, s] = reply
        for going, _ in r_moves[e]:
            going.start()
        rarr[e, me] = rsend[e, me]
        if e == 0:
            chi, clo = twin(cw[0]), twin(cw[1])
            full = split(dot3((lw[0], lw[1]), (chi, clo), 1))
            for part in range(2):
                for c in range(CAP):
                    for p in range(2):
                        begin = (p * CAP + c) * wide
                        m2[part, c, :, p * wide:(p + 1) * wide] = full[part][:, begin:begin + wide]
            prepare(1)
        for _, into in r_moves[e]:
            into.wait_recv()
        w = rarr[e].reshape(wide, width)
        w_hi, w_lo = split(jnp.concatenate([w, turned(w, cols)], axis=0))
        w_both = jnp.concatenate([w_hi, w_lo], axis=1)

        def corrected(rows):
            parts = []
            for c in range(CAP):
                p = mm(m2[0, c, rows], w_both)
                parts.append(p[:, :width] + p[:, width:] + mm(m2[1, c, rows], w_hi))
            return ybuf[e, rows] + folded(pick(parts, lanes), lanes)

        def pass_on():
            rows = pl.ds(pl.multiple_of((1 - d) * (psize - tsize), 8), tsize)
            trace = corrected(rows)
            tsend[d] = pick([trace[:tsize // 2], trace[tsize // 2:]], lanes)
            trace_move(e).start()

        if e == 0:
            pass_on()
        else:
            pl.when(inner)(pass_on)
        out[d] = corrected(pl.ds(0, psize)).T[:lanes].reshape(2, cols, psize)

    for moves in [mask_moves] + u_moves + r_moves:
        for going, _ in moves:
            going.wait_send()
    trace_move(0).wait_send()

    @pl.when(inner)
    def _():
        trace_move(1).wait_send()


def solution(mesh):
    leaves, depth = mesh.shape["front"], mesh.shape["layer"]

    def body(s_down, s_up, leaf, coup, sep, j_top, j_bot, targets, offsets):
        cols, psize = s_down.shape[3:]
        nb = offsets.shape[2]
        bsize, qsize, tsize = coup.shape[3], sep.shape[3], j_top.shape[3]
        rb = bsize // nb
        qb = qsize // rb
        lanes = 2 * cols
        width = CAP * lanes
        rows = leaves * CAP * rb
        vmem = pl.BlockSpec(memory_space=pltpu.VMEM)
        smem = pl.BlockSpec(memory_space=pltpu.SMEM)
        sems = pltpu.SemaphoreType.DMA
        fields = pl.pallas_call(
            functools.partial(kernel, leaves, depth),
            out_shape=jax.ShapeDtypeStruct((2, 2, cols, psize), F32),
            in_specs=[smem] * 2 + [vmem] * 4 + [pl.BlockSpec(memory_space=pl.ANY)] * 3,
            out_specs=vmem,
            scratch_shapes=[
                pltpu.VMEM((2, qsize, qsize), F32),
                pltpu.VMEM((2, tsize, psize), F32),
                pltpu.VMEM((2, tsize, psize), F32),
                pltpu.VMEM((2, psize, 2 * psize), BF16),
                pltpu.VMEM((2, rows, 2 * psize), BF16),
                pltpu.VMEM((2, qsize, 2 * qsize), BF16),
                pltpu.VMEM((2, 2, psize, 2 * tsize), BF16),
                pltpu.VMEM((2, 2, rows, 2 * tsize), BF16),
                pltpu.VMEM((2, CAP, psize, 2 * leaves * rb), BF16),
                pltpu.VMEM((2, psize, width), F32),
                pltpu.VMEM((2, leaves * rb, width), F32),
                pltpu.VMEM((leaves, qb, width), F32),
                pltpu.VMEM((leaves, qb, width), F32),
                pltpu.VMEM((2, leaves, rb, width), F32),
                pltpu.VMEM((2, leaves, rb, width), F32),
                pltpu.VMEM((2, leaves, rb, width), F32),
                pltpu.VMEM((2, leaves, rb, width), F32),
                pltpu.VMEM((2, tsize // 2, 2 * lanes), F32),
                pltpu.VMEM((2, tsize // 2, 2 * lanes), F32),
                sems((3,)),
                sems((leaves,)), sems((leaves,)),
                sems((2, leaves)), sems((2, leaves)),
                sems((2, leaves)), sems((2, leaves)),
                sems((2,)), sems((2,)),
            ],
            compiler_params=pltpu.CompilerParams(
                collective_id=0, has_side_effects=True, vmem_limit_bytes=56 * 1024 * 1024
            ),
        )(
            targets.reshape(nb), offsets.reshape(nb),
            s_down[0, 0], s_up[0, 0], leaf[0, 0], coup[0, 0].reshape(2, nb, rb, psize),
            sep[0, 0], j_top[0, 0], j_bot[0, 0],
        )
        return fields[0][None, None], fields[1][None, None]

    five, four, three = (P("layer", "front", *([None] * k)) for k in (3, 2, 1))
    return jax.shard_map(
        body, mesh=mesh, in_specs=(five,) * 7 + (four, three), out_specs=(five, five), check_vma=False
    )
```
